32 devices in a mesh: grp: 2 (over x), sky: 16 (over z, y, core).
Axes of the slice: x: 2, y: 2, z: 4, core: 2. Of those that a mesh axis runs over, the one named last changes fastest.
Arguments:
- section_image: bfloat16 [16384, 512], P(('grp', 'sky')), parts along dimension 0, may hold values from -6 to 6
- mask_plane: int32 [16384, 512], P(('grp', 'sky')), parts along dimension 0, may hold values from 0 to 65279
- visit_weight: float32 [32], P(('grp', 'sky')), parts along dimension 0, may hold values from 0.5 to 4
- poly_coeff: float32 [32, 12, 6], P(('grp', 'sky')), parts along dimension 0, may hold values from -1.5 to 1.5
- shift_phase: int32 [32, 2], P(('grp', 'sky')), parts along dimension 0, may hold values from 0 to 31
- piece_rows: int32 [32, 4], P(('grp', 'sky')), parts along dimension 0, may hold values from 1 to 256, 512 in all within a row
- piece_start: int32 [32, 4], P('grp'), parts along dimension 0, may hold values from 0 to 256, as said below
- basis_vertical: float32 [12, 21], replicated, may hold values from -1.25 to 1.25
- basis_horizontal: float32 [12, 21], replicated, may hold values from -1.25 to 1.25
Outputs:
- coadd: float32 [16384, 512], P(('grp', 'sky')), parts along dimension 0
- detection: float32 [5, 16384, 512], P(None, ('grp', 'sky')), parts along dimension 1
The draws below stay inside these ranges and needn't reach their ends.
There are 2 independent parts, one for each index of `grp`. The reference program is written for one: setup_inputs(seed, part) draws one part's arguments, and reference() takes and returns one part's arrays. A program takes and returns all parts, laid end to end along the dimension named above; an argument that names none is the same for every part. Nothing has to cross between parts.
Inputs may be any that keep to these rules, and one draw needn't show every extreme that they name: `piece_rows`: for each section the 4 counts sum to 512, and one of them is exactly 256. `piece_start`: both ends of the range occur in every draw.
All inputs are finite; a program needn't handle non-finite values.
Results may differ from the reference program's by a relative error of at most 0.0008.
The reference program's roundings to bfloat16 on the way count: a program that leaves them out, or rounds other values in their place, can miss the bound.
Values may be sent and summed in bfloat16 or wider, within the bound.
A program may use at most 64 MiB of HBM per device.

```python
import math
import jax
import jax.numpy as jnp
import numpy as np
from jax import lax

C = 512
SEC_R = 512
W = 4
NB = 12
TAPS = 21
NPOLY = 6
LTAPS = 6
PHASES = 32
HALO = 16
NSCALE = 5
CAP = 256
SECTIONS = 16
ROWS = 8192


def draw_piece_start(key, part):
    highest = SEC_R - CAP
    total_slots = SECTIONS * W
    values = jax.random.randint(key, (total_slots,), 0, highest + 1)
    top_slot = jax.random.randint(jax.random.fold_in(key, 1), (), 0, total_slots)
    other_gap = jax.random.randint(jax.random.fold_in(key, 2), (), 0, total_slots - 1)
    low_slot = jnp.remainder(top_slot + 1 + other_gap, total_slots)
    values = values.at[top_slot].set(highest)
    values = values.at[low_slot].set(0)
    return values.reshape(SECTIONS, W).astype(jnp.int32)


def plant(entries, stream_key, least, high):
    spot = [jax.random.randint(jax.random.fold_in(stream_key, axis), (), 0, length) for axis, length in enumerate(entries.shape)]
    longest = entries.shape.index(max(entries.shape))
    beside = spot[:longest] + [(spot[longest] + 1) % entries.shape[longest]] + spot[longest + 1:]
    return entries.at[tuple(spot)].set(least).at[tuple(beside)].set(high)


def block_levels(rng, shape, pieces, low, high):
    gain = 1.0
    for axis_at, blocks in pieces:
        steps = jax.random.uniform(jax.random.fold_in(jax.random.fold_in(rng, 6), axis_at), (blocks,), jnp.float32, low / len(pieces), high / len(pieces))
        gain = gain * jnp.repeat(jnp.exp(steps), shape[axis_at] // blocks).reshape((-1,) + (1,) * (len(shape) - 1 - axis_at))
    return gain


def length_profile(number_of, total, limit, skew):
    weights = [(1 << 20) // math.isqrt(rank ** skew) + 1 for rank in range(2, number_of + 1)]
    spare, holding = total - limit - (number_of - 1), [1] * (number_of - 1)
    while spare > 0:
        movable = [i for i in range(number_of - 1) if holding[i] < limit]
        mass, budget = sum([weights[i] for i in movable]), spare
        for i in movable:
            more = min(limit - holding[i], max(1, budget * weights[i] // mass), spare)
            holding[i] = holding[i] + more
            spare = spare - more
    return np.array([limit] + holding)


def uneven(stream_key, count, total, bound, lean):
    if count == 2:
        one = jax.random.randint(stream_key, (), max(1, total - bound), min(bound, total - 1) + 1)
        return jnp.stack([one, total - one])
    sizes = jnp.asarray(length_profile(count, total, bound, lean), jnp.int32)
    twos = (count - 1) // 2
    donor, taker = sizes[1:1 + 2 * twos:2], sizes[2:2 + 2 * twos:2]
    room = jnp.minimum(donor - 1, bound - taker)
    passed = jax.random.randint(jax.random.fold_in(stream_key, 1), (twos,), 0, 1 << 20) % (room + 1)
    sizes = sizes.at[1:1 + 2 * twos:2].set(donor - passed).at[2:2 + 2 * twos:2].set(taker + passed)
    return sizes[jax.random.permutation(jax.random.fold_in(stream_key, 2), count)]


def normal_values(rng, shape, deviation, limit, pieces=(), kind=jnp.bfloat16):
    drawn = deviation * jax.random.normal(rng, shape, jnp.float32)
    if pieces:
        drawn = drawn * block_levels(rng, shape, pieces, -0.22, 0.18)
    return jnp.clip(drawn, -limit, limit).astype(kind)


def setup_inputs(seed: int = 0, part: int = 0) -> dict:
    arg_keys = jax.random.split(jax.random.key(seed), 10)
    part_splits = jax.random.split(jax.random.fold_in(arg_keys[9], part), 10)
    return {
        "section_image": normal_values(part_splits[0], (ROWS, C), 1.0, 6.0, ((0, 16),)),
        "mask_plane": plant(jax.random.randint(part_splits[1], (ROWS, C), 0, 65280), jax.random.fold_in(part_splits[1], 1), 0, 65279).astype(jnp.int32),
        "visit_weight": jnp.clip(jnp.exp(math.log(4.0) - 2.0794415 * jax.random.uniform(part_splits[2], (SECTIONS,), jnp.float32) ** block_levels(part_splits[2], (SECTIONS,), ((0, 16),), -0.2, 0.2)), 0.5, 4.0),
        "poly_coeff": normal_values(part_splits[3], (SECTIONS, NB, NPOLY), 0.25, 1.5, ((0, 16),), jnp.float32),
        "shift_phase": plant(jax.random.randint(part_splits[4], (SECTIONS, 2), 0, PHASES), jax.random.fold_in(part_splits[4], 1), 0, PHASES - 1).astype(jnp.int32),
        "piece_rows": jax.vmap(lambda own: uneven(own, W, SEC_R, CAP, 2))(jax.random.split(part_splits[5], SECTIONS)).reshape((SECTIONS, W)).astype(jnp.int32),
        "piece_start": draw_piece_start(jax.random.fold_in(jax.random.fold_in(arg_keys[9], part), 71), part),
        "basis_vertical": normal_values(arg_keys[7], (NB, TAPS), TAPS ** -0.5, 1.25, (), jnp.float32),
        "basis_horizontal": normal_values(arg_keys[8], (NB, TAPS), TAPS ** -0.5, 1.25, (), jnp.float32),
    }


def rounded(values):
    return lax.optimization_barrier(values.astype(jnp.bfloat16)).astype(jnp.float32)


def slide_sum(values, tap_values, center, axis_index):
    extent = values.shape[axis_index]
    tap_count = tap_values.shape[0]
    pad_width = [(0, 0), (0, 0)]
    pad_width[axis_index] = (center, tap_count - 1 - center)
    padded = jnp.pad(values, pad_width)
    running = jnp.zeros(values.shape, jnp.float32)
    for position in range(tap_count):
        sliced = lax.slice_in_dim(padded, position, position + extent, axis=axis_index)
        running = running + tap_values[position] * sliced
    return running


def lanczos_taps(phase_value):
    fraction = phase_value.astype(jnp.float32) / PHASES
    tap_offsets = jnp.arange(LTAPS).astype(jnp.float32) - (LTAPS // 2 - 1) - fraction
    values = jnp.sinc(tap_offsets) * jnp.sinc(tap_offsets / 3.0)
    return values / jnp.sum(values)


def warp_section(pixels, mask_rows, weight_value, coeffs, phases, vert_taps, horiz_taps):
    row_count, col_count = pixels.shape
    half_width = (vert_taps.shape[1] - 1) // 2
    row_coord = 2.0 * jnp.arange(row_count).astype(jnp.float32)[:, None] / (row_count - 1) - 1.0
    col_coord = 2.0 * jnp.arange(col_count).astype(jnp.float32)[None, :] / (col_count - 1) - 1.0
    pixels_wide = pixels.astype(jnp.float32)

    def one_basis(matched, inputs):
        vert_one, horiz_one, factor = inputs
        vertical = rounded(slide_sum(pixels_wide, vert_one, half_width, 0))
        horizontal = slide_sum(vertical, horiz_one, half_width, 1)
        weight = (factor[0] + factor[1] * row_coord + factor[2] * col_coord + factor[3] * row_coord * row_coord
                  + factor[4] * row_coord * col_coord + factor[5] * col_coord * col_coord)
        return matched + weight * horizontal, None

    matched, _ = lax.scan(one_basis, jnp.zeros((row_count, col_count), jnp.float32), (vert_taps, horiz_taps, coeffs))
    matched = rounded(matched)
    tap_lead = LTAPS // 2 - 1
    row_taps = rounded(lanczos_taps(phases[0]))
    col_taps = rounded(lanczos_taps(phases[1]))
    row_shifted = rounded(slide_sum(matched, row_taps, tap_lead, 0))
    warped = slide_sum(row_shifted, col_taps, tap_lead, 1)
    kept_pixel = jnp.remainder(mask_rows, 8) != 0
    pixel_weight = jnp.where(kept_pixel, weight_value, jnp.float32(0.0))
    return (pixel_weight * warped).astype(jnp.bfloat16), pixel_weight.astype(jnp.bfloat16)


def reference(section_image, mask_plane, visit_weight, poly_coeff, shift_phase, piece_rows, piece_start, basis_vertical, basis_horizontal):
    sections = visit_weight.shape[0]
    row_count = section_image.shape[0] // sections
    col_count = section_image.shape[1]
    piece_count = piece_rows.shape[1]
    capacity = 2 * row_count // piece_count
    vert_taps = rounded(basis_vertical)
    horiz_taps = rounded(basis_horizontal)
    images = section_image.reshape(sections, row_count, col_count)
    mask_stack = mask_plane.reshape(sections, row_count, col_count)

    def warp_one(inputs):
        pixels, mask_rows, weight_value, coeffs, phases = inputs
        return warp_section(pixels, mask_rows, weight_value, coeffs, phases, vert_taps, horiz_taps)

    flux_all, weight_all = lax.map(warp_one, (images, mask_stack, visit_weight, poly_coeff, shift_phase))
    tail_zeros = jnp.zeros((sections, capacity, col_count), jnp.bfloat16)
    flux_pad = jnp.concatenate([flux_all, tail_zeros], axis=1)
    weight_pad = jnp.concatenate([weight_all, tail_zeros], axis=1)
    begins = (jnp.cumsum(piece_rows, axis=1) - piece_rows).astype(jnp.int32)
    slot_rows = jnp.arange(capacity).astype(jnp.int32)[:, None]

    def gather_patch(owner_index):
        flux_sum = jnp.zeros((row_count, col_count), jnp.float32)
        weight_sum = jnp.zeros((row_count, col_count), jnp.float32)
        for offset in range(piece_count):
            source = jnp.remainder(owner_index - offset + sections, sections).astype(jnp.int32)
            begin_row = begins[source, offset].astype(jnp.int32)
            rows_live = piece_rows[source, offset]
            start_row = piece_start[source, offset].astype(jnp.int32)
            live_rows = slot_rows < rows_live
            flux_piece = jnp.where(live_rows, lax.dynamic_slice_in_dim(flux_pad[source], begin_row, capacity, 0).astype(jnp.float32), jnp.float32(0.0))
            weight_piece = jnp.where(live_rows, lax.dynamic_slice_in_dim(weight_pad[source], begin_row, capacity, 0).astype(jnp.float32), jnp.float32(0.0))
            flux_sum = lax.dynamic_update_slice_in_dim(flux_sum, lax.dynamic_slice_in_dim(flux_sum, start_row, capacity, 0) + flux_piece, start_row, 0)
            weight_sum = lax.dynamic_update_slice_in_dim(weight_sum, lax.dynamic_slice_in_dim(weight_sum, start_row, capacity, 0) + weight_piece, start_row, 0)
        return flux_sum / (1.0 + weight_sum)

    coadd = lax.map(gather_patch, jnp.arange(sections).astype(jnp.int32)).reshape(sections * row_count, col_count)
    total_rows = sections * row_count
    wrapped = jnp.concatenate([coadd[total_rows - HALO:], coadd, coadd[:HALO]], axis=0)
    tap_offsets = jnp.arange(-HALO, HALO + 1).astype(jnp.float32)
    scale_maps = []
    for scale_index in range(NSCALE):
        kernel_width = HALO * (scale_index + 1) / (2.0 * NSCALE)
        gaussian = jnp.exp(-tap_offsets * tap_offsets / (2.0 * kernel_width * kernel_width))
        gaussian = gaussian / jnp.sum(gaussian)
        norm_factor = 1.0 / jnp.sum(gaussian * gaussian)
        smoothed_rows = slide_sum(wrapped, gaussian, 0, 0)[:total_rows]
        scale_maps.append(norm_factor * slide_sum(smoothed_rows, gaussian, HALO, 1))
    return coadd, jnp.stack(scale_maps)
```

```python
import functools

import jax
import jax.numpy as jnp
import numpy as np
from jax import lax
from jax.experimental import pallas as pl
from jax.experimental.pallas import tpu as pltpu
from jax.sharding import PartitionSpec as P

LTAPS = 6
PHASES = 32
HALO = 16
NSCALE = 5
RB = 128
MARGIN = 64
F32 = jnp.float32
BF16 = jnp.bfloat16
VMEM = pltpu.VMEM
LIMIT = 60 * 1024 * 1024


def dot(a, b):
    return jnp.dot(a, b, preferred_element_type=F32)


def lanczos_table():
    phase = np.arange(PHASES)[:, None] / PHASES
    offsets = np.arange(LTAPS)[None, :] - (LTAPS // 2 - 1) - phase
    values = np.sinc(offsets) * np.sinc(offsets / 3.0)
    return values / values.sum(1, keepdims=True)


def padded_rows(values, width, shift):
    lead = shift % 8
    return jnp.pad(values, ((0, 0), (lead, width - lead - values.shape[1])))


def toeplitz(row, rows, shift):
    wide = jnp.broadcast_to(row, (rows, row.shape[1]))
    return pltpu.roll(wide, shift // 8 * 8 % row.shape[1], 1, stride=1, stride_axis=0)


def fill_column_band(band_ref, circulant, reach):
    half = circulant.shape[0]
    gap = lax.broadcasted_iota(jnp.int32, (half, half), 1) - lax.broadcasted_iota(
        jnp.int32, (half, half), 0
    )
    zero = jnp.zeros_like(circulant)
    upper = jnp.where(gap <= reach - half, circulant, zero).astype(BF16)
    lower = jnp.where(gap >= half - reach, circulant, zero).astype(BF16)
    diag = jnp.where(jnp.abs(gap) <= reach, circulant, zero).astype(BF16)
    count = band_ref.shape[0] // half
    none = jnp.zeros((half, half), BF16)
    for a in range(count):
        for b in range(count):
            tile = diag if a == b else upper if b == a + 1 else lower if b == a - 1 else none
            band_ref[a * half : (a + 1) * half, b * half : (b + 1) * half] = tile


def send_slots(rows_ref, plane, outs):
    cap, rows = outs[0].shape[0], plane.shape[0]
    row = lax.broadcasted_iota(jnp.int32, (cap, rows), 0)
    gap = lax.broadcasted_iota(jnp.int32, (cap, rows), 1) - row
    begin = 0
    for o, out in enumerate(outs):
        live = rows_ref[0, o]
        pick = jnp.where((row < live) & (gap == begin), 1.0, 0.0).astype(BF16)
        out[...] = dot(pick, plane).astype(BF16)
        begin = begin + live


def weight_kernel(vw_ref, rows_ref, mask_ref, *outs):
    plane = jnp.where((mask_ref[...] & 7) != 0, vw_ref[0], 0.0).astype(BF16)
    send_slots(rows_ref, plane, outs)


def warp_kernel(taps, vw_ref, coeff_ref, phase_ref, rows_ref, img_ref, mask_ref, vt_ref, ht_ref,
                lrow_ref, lcol_ref, *refs):
    outs, (xpad, vert, band, tall, acc) = refs[:-5], refs[-5:]
    rows, cols = img_ref.shape
    bases = vt_ref.shape[0]
    half_width = taps // 2
    blocks = rows // RB
    window = RB + 2 * MARGIN
    xpad[:MARGIN, :] = jnp.zeros((MARGIN, cols), BF16)
    xpad[rows + MARGIN :, :] = jnp.zeros((MARGIN, cols), BF16)
    xpad[MARGIN : rows + MARGIN, :] = img_ref[...]
    acc[...] = jnp.zeros_like(acc)
    for k in range(bases):
        tall[k * RB : (k + 1) * RB, :] = toeplitz(
            vt_ref[k : k + 1, :], RB, MARGIN - half_width
        ).astype(BF16)
    for b in range(blocks):
        for k in range(bases):
            vert[k, b * RB : (b + 1) * RB, :] = dot(
                tall[k * RB : (k + 1) * RB, :], xpad[b * RB : b * RB + window, :]
            ).astype(BF16)
    u = 2.0 * lax.broadcasted_iota(jnp.int32, (rows, 128), 0).astype(F32) / (rows - 1) - 1.0

    def one_basis(k, _):
        circulant = toeplitz(ht_ref[pl.ds(k, 1), :], ht_ref.shape[1], -(taps - 1 - half_width))
        fill_column_band(band, circulant, half_width)
        row_part = coeff_ref[k, 0] + u * (coeff_ref[k, 1] + u * coeff_ref[k, 3])
        cross = coeff_ref[k, 2] + u * coeff_ref[k, 4]
        for lane in range(0, cols, 256):
            horizontal = dot(vert[k], band[:, lane : lane + 256])
            for part in range(0, 256, 128):
                at = lane + part
                v = (
                    2.0 * (lax.broadcasted_iota(jnp.int32, (1, 128), 1) + at).astype(F32)
                    / (cols - 1)
                    - 1.0
                )
                weight = row_part + cross * v + coeff_ref[k, 5] * (v * v)
                acc[:, at : at + 128] += weight * horizontal[:, part : part + 128]
        return 0

    lax.fori_loop(0, bases, one_basis, 0)
    xpad[MARGIN : rows + MARGIN, :] = acc[...].astype(BF16)
    lead = LTAPS // 2 - 1
    row_band = toeplitz(lrow_ref[pl.ds(phase_ref[0, 0], 1), :], RB, MARGIN - lead).astype(BF16)
    for b in range(blocks):
        vert[0, b * RB : (b + 1) * RB, :] = dot(row_band, xpad[b * RB : b * RB + window, :]).astype(
            BF16
        )
    circulant = toeplitz(
        lcol_ref[pl.ds(phase_ref[0, 1], 1), :], lcol_ref.shape[1], -(LTAPS - 1 - lead)
    )
    fill_column_band(band, circulant, LTAPS - 1 - lead)
    warped = dot(vert[0], band[...])
    weight = jnp.where((mask_ref[...] & 7) != 0, vw_ref[0], 0.0)
    send_slots(rows_ref, (weight * warped).astype(BF16), outs)


def coadd_kernel(count, start_ref, *refs):
    flux, weight, out_ref = refs[:count], refs[count : 2 * count], refs[2 * count]
    cap, rows = flux[0].shape[0], out_ref.shape[0]
    gap = lax.broadcasted_iota(jnp.int32, (rows, cap), 0) - lax.broadcasted_iota(
        jnp.int32, (rows, cap), 1
    )
    flux_sum = weight_sum = 0.0
    for o in range(count):
        put = jnp.where(gap == start_ref[o], 1.0, 0.0).astype(BF16)
        flux_sum += dot(put, flux[o][...])
        weight_sum += dot(put, weight[o][...])
    out_ref[...] = flux_sum / (1.0 + weight_sum)


def detect_kernel(co_ref, lo_ref, hi_ref, grow_ref, ghi_ref, glo_ref, out_ref, tall, stack, smooth,
                  band_hi, band_lo):
    q = pl.program_id(0)
    rows, cols = co_ref.shape
    window = RB + 2 * HALO
    blocks = rows // RB

    @pl.when(q == 0)
    def _():
        for s in range(NSCALE):
            tall[s * RB : (s + 1) * RB, :] = toeplitz(grow_ref[s : s + 1, :], RB, 0).astype(BF16)
        stack[3 * window :, :] = jnp.zeros((stack.shape[0] - 3 * window, cols), BF16)
        for b in range(blocks):
            top = lo_ref[...] if b == 0 else co_ref[b * RB - HALO : b * RB, :]
            end = (b + 1) * RB
            bottom = hi_ref[...] if b == blocks - 1 else co_ref[end : end + HALO, :]
            for at, part in ((0, top), (HALO, co_ref[b * RB : end, :]), (HALO + RB, bottom)):
                coarse = part.astype(BF16)
                fine = (part - coarse.astype(F32)).astype(BF16)
                size = part.shape[0]
                stack[at : at + size, :] = coarse
                stack[window + at : window + at + size, :] = fine
                stack[2 * window + at : 2 * window + at + size, :] = coarse
            for s in range(NSCALE):
                result = dot(tall[s * RB : (s + 1) * RB, :], stack[...])
                coarse = result.astype(BF16)
                smooth[s, b * RB : end, :cols] = coarse
                smooth[s, b * RB : end, cols:] = (result - coarse.astype(F32)).astype(BF16)

    for g_ref, band in ((ghi_ref, band_hi), (glo_ref, band_lo)):
        fill_column_band(
            band, toeplitz(g_ref[pl.ds(q, 1), :], g_ref.shape[1], -HALO), HALO
        )
    for lane in range(0, cols, 256):
        part = slice(lane, lane + 256)
        out_ref[:, part] = (
            dot(smooth[q, :, :cols], band_hi[:, part])
            + dot(smooth[q, :, cols:], band_hi[:, part])
            + dot(smooth[q, :, :cols], band_lo[:, part])
        )


def split_np(values):
    import ml_dtypes

    values = values.astype(np.float32)
    coarse = values.astype(ml_dtypes.bfloat16).astype(np.float32)
    return coarse, values - coarse


def vm(count):
    return [pl.BlockSpec(memory_space=pltpu.VMEM)] * count


def sm(count):
    return [pl.BlockSpec(memory_space=pltpu.SMEM)] * count


def shifted(x, by):
    peers = lax.axis_size("sky")
    return lax.ppermute(x, "sky", [(i, (i + by) % peers) for i in range(peers)])


def body(
    section_image,
    mask_plane,
    visit_weight,
    poly_coeff,
    shift_phase,
    piece_rows,
    piece_start,
    basis_vertical,
    basis_horizontal,
):
    rows, cols = section_image.shape
    pieces = piece_rows.shape[1]
    cap = 2 * rows // pieces
    bases, taps = basis_vertical.shape
    slot = jax.ShapeDtypeStruct((cap, cols), BF16)
    params = pltpu.CompilerParams(vmem_limit_bytes=LIMIT)

    weights = pl.pallas_call(
        weight_kernel,
        name="weight_slots",
        out_shape=[slot] * pieces,
        in_specs=sm(2) + vm(1),
        out_specs=vm(pieces),
        compiler_params=params,
    )(visit_weight, piece_rows, mask_plane)
    weights = [weights[0]] + [shifted(weights[o], o) for o in range(1, pieces)]

    vert_rows = padded_rows(basis_vertical.astype(BF16).astype(F32), RB + 2 * MARGIN, MARGIN - taps // 2)
    horiz_rows = padded_rows(basis_horizontal.astype(BF16).astype(F32)[:, ::-1], 256, taps // 2 + 1 - taps)
    table = lanczos_table().astype(np.float32)
    lead = LTAPS // 2 - 1
    lan_row = padded_rows(
        jnp.asarray(table).astype(BF16).astype(F32), RB + 2 * MARGIN, MARGIN - lead
    )
    lan_col = padded_rows(
        jnp.asarray(table[:, ::-1]).astype(BF16).astype(F32), 256, lead + 1 - LTAPS
    )
    fluxes = pl.pallas_call(
        functools.partial(warp_kernel, taps),
        name="warp",
        out_shape=[slot] * pieces,
        in_specs=sm(4) + vm(6),
        out_specs=vm(pieces),
        scratch_shapes=[
            VMEM((rows + 2 * MARGIN, cols), BF16),
            VMEM((bases, rows, cols), BF16),
            VMEM((cols, cols), BF16),
            VMEM((bases * RB, RB + 2 * MARGIN), BF16),
            VMEM((rows, cols), F32),
        ],
        compiler_params=params,
        cost_estimate=pl.CostEstimate(
            flops=4 * bases * rows * cols * cols, bytes_accessed=4 * rows * cols, transcendentals=0
        ),
    )(visit_weight, poly_coeff[0], shift_phase, piece_rows, section_image, mask_plane, vert_rows,
      horiz_rows, lan_row, lan_col)
    fluxes = [fluxes[0]] + [shifted(fluxes[o], o) for o in range(1, pieces)]

    me = lax.axis_index("sky")
    peers = lax.axis_size("sky")
    starts = jnp.stack([piece_start[jnp.remainder(me - o + peers, peers), o] for o in range(pieces)])
    coadd = pl.pallas_call(
        functools.partial(coadd_kernel, pieces),
        name="coadd",
        out_shape=jax.ShapeDtypeStruct((rows, cols), F32),
        in_specs=sm(1) + vm(2 * pieces),
        out_specs=pl.BlockSpec(memory_space=pltpu.VMEM),
        compiler_params=params,
    )(starts, *fluxes, *weights)

    low = shifted(coadd[rows - HALO :], 1)
    high = shifted(coadd[:HALO], -1)
    offsets = np.arange(-HALO, HALO + 1)
    window = RB + 2 * HALO
    row_taps = np.zeros((NSCALE, 512), np.float32)
    col_hi = np.zeros((NSCALE, 256), np.float32)
    col_lo = np.zeros((NSCALE, 256), np.float32)
    count = 2 * HALO + 1
    for q in range(NSCALE):
        width = HALO * (q + 1) / (2.0 * NSCALE)
        gaussian = np.exp(-offsets * offsets / (2.0 * width * width))
        gaussian = gaussian / gaussian.sum()
        coarse, fine = split_np(gaussian)
        row_taps[q, :count] = coarse
        row_taps[q, window : window + count] = coarse
        row_taps[q, 2 * window : 2 * window + count] = fine
        col_hi[q, :count], col_lo[q, :count] = split_np(gaussian / (gaussian * gaussian).sum())
    whole = lambda shape: pl.BlockSpec(shape, lambda q: (0, 0))
    detection = pl.pallas_call(
        detect_kernel,
        name="detect",
        grid=(NSCALE,),
        out_shape=jax.ShapeDtypeStruct((NSCALE, rows, cols), F32),
        in_specs=[
            whole((rows, cols)),
            whole((HALO, cols)),
            whole((HALO, cols)),
            whole((NSCALE, 512)),
            whole((NSCALE, 256)),
            whole((NSCALE, 256)),
        ],
        out_specs=pl.BlockSpec((None, rows, cols), lambda q: (q, 0, 0)),
        scratch_shapes=[
            VMEM((NSCALE * RB, 512), BF16),
            VMEM((512, cols), BF16),
            VMEM((NSCALE, rows, 2 * cols), BF16),
            VMEM((cols, cols), BF16),
            VMEM((cols, cols), BF16),
        ],
        compiler_params=params,
    )(coadd, low, high, jnp.asarray(row_taps), jnp.asarray(col_hi), jnp.asarray(col_lo))
    return coadd, detection


def solution(mesh):
    return jax.shard_map(
        body,
        mesh=mesh,
        in_specs=(
            P(("grp", "sky"), None),
            P(("grp", "sky"), None),
            P(("grp", "sky")),
            P(("grp", "sky"), None, None),
            P(("grp", "sky"), None),
            P(("grp", "sky"), None),
            P("grp", None),
            P(),
            P(),
        ),
        out_specs=(P(("grp", "sky"), None), P(None, ("grp", "sky"), None)),
        check_vma=False,
    )
```

```python
import functools

import jax
import jax.numpy as jnp
import ml_dtypes
import numpy as np
from jax import lax
from jax.experimental import pallas as pl
from jax.experimental.pallas import tpu as pltpu
from jax.sharding import PartitionSpec as P

LTAPS = 6
PHASES = 32
HALO = 16
NSCALE = 5
RB = 128
MARGIN = 64
F32 = jnp.float32
BF16 = jnp.bfloat16
VMEM = pltpu.VMEM
LIMIT = 60 * 1024 * 1024


def dot(a, b):
    return jnp.dot(a, b, preferred_element_type=F32)


def lanczos_table():
    phase = np.arange(PHASES)[:, None] / PHASES
    offsets = np.arange(LTAPS)[None, :] - (LTAPS // 2 - 1) - phase
    values = np.sinc(offsets) * np.sinc(offsets / 3.0)
    return values / values.sum(1, keepdims=True)


def padded_rows(values, width, shift):
    lead = shift % 8
    return np.pad(values, ((0, 0), (lead, width - lead - values.shape[1])))


def toeplitz(row, rows, shift):
    wide = jnp.broadcast_to(row, (rows, row.shape[1]))
    return pltpu.roll(wide, shift // 8 * 8 % row.shape[1], 1, stride=1, stride_axis=0)


def fill_column_band(band_ref, circulant, reach):
    half = circulant.shape[0]
    gap = lax.broadcasted_iota(jnp.int32, (half, half), 1) - lax.broadcasted_iota(
        jnp.int32, (half, half), 0
    )
    zero = jnp.zeros_like(circulant)
    upper = jnp.where(gap <= reach - half, circulant, zero).astype(BF16)
    lower = jnp.where(gap >= half - reach, circulant, zero).astype(BF16)
    diag = jnp.where(jnp.abs(gap) <= reach, circulant, zero).astype(BF16)
    count = band_ref.shape[0] // half
    none = jnp.zeros((half, half), BF16)
    for a in range(count):
        for b in range(count):
            tile = diag if a == b else upper if b == a + 1 else lower if b == a - 1 else none
            band_ref[a * half : (a + 1) * half, b * half : (b + 1) * half] = tile


def send_slots(rows_ref, plane, outs):
    cap, rows = outs[0].shape[0], plane.shape[0]
    row = lax.broadcasted_iota(jnp.int32, (cap, rows), 0)
    gap = lax.broadcasted_iota(jnp.int32, (cap, rows), 1) - row
    begin = 0
    for o, out in enumerate(outs):
        live = rows_ref[0, o]
        pick = jnp.where((row < live) & (gap == begin), 1.0, 0.0).astype(BF16)
        out[...] = dot(pick, plane).astype(BF16)
        begin = begin + live


def weight_kernel(vw_ref, rows_ref, mask_ref, *outs):
    plane = jnp.where((mask_ref[...] & 7) != 0, vw_ref[0], 0.0).astype(BF16)
    send_slots(rows_ref, plane, outs)


def spread_taps(raw_ref, pad_ref, out_ref, lead, step):
    count, taps = raw_ref.shape
    pad_ref[...] = jnp.zeros_like(pad_ref)
    pad_ref[:count, :taps] = raw_ref[...]
    shape = (pad_ref.shape[1], out_ref.shape[1])
    tap = lax.broadcasted_iota(jnp.int32, shape, 0)
    lane = lax.broadcasted_iota(jnp.int32, shape, 1)
    pick = jnp.where((lane == lead + step * tap) & (tap < taps), 1.0, 0.0).astype(BF16)
    out_ref[...] = dot(pad_ref[...].astype(BF16), pick)


def warp_kernel(vw_ref, coeff_ref, phase_ref, rows_ref, _, img_ref, mask_ref, rawv_ref, rawh_ref,
                lrow_ref, lcol_ref, *refs):
    outs, (xpad, vert, band, tall, acc, pad, vt_ref, ht_ref) = refs[:-8], refs[-8:]
    bases, taps = rawv_ref.shape
    rows, cols = img_ref.shape
    half_width = taps // 2
    spread_taps(rawv_ref, pad, vt_ref, (MARGIN - half_width) % 8, 1)
    spread_taps(rawh_ref, pad, ht_ref, (half_width + 1 - taps) % 8 + taps - 1, -1)
    blocks = rows // RB
    window = RB + 2 * MARGIN
    xpad[:MARGIN, :] = jnp.zeros((MARGIN, cols), BF16)
    xpad[rows + MARGIN :, :] = jnp.zeros((MARGIN, cols), BF16)
    xpad[MARGIN : rows + MARGIN, :] = img_ref[...]
    acc[...] = jnp.zeros_like(acc)
    for k in range(bases):
        tall[k * RB : (k + 1) * RB, :] = toeplitz(
            vt_ref[k : k + 1, :], RB, MARGIN - half_width
        ).astype(BF16)
    for b in range(blocks):
        for k in range(bases):
            vert[k, b * RB : (b + 1) * RB, :] = dot(
                tall[k * RB : (k + 1) * RB, :], xpad[b * RB : b * RB + window, :]
            ).astype(BF16)
    u = 2.0 * lax.broadcasted_iota(jnp.int32, (rows, 128), 0).astype(F32) / (rows - 1) - 1.0

    def one_basis(k, _):
        circulant = toeplitz(ht_ref[pl.ds(k, 1), :], ht_ref.shape[1], -(taps - 1 - half_width))
        fill_column_band(band, circulant, half_width)
        row_part = coeff_ref[0, k, 0] + u * (coeff_ref[0, k, 1] + u * coeff_ref[0, k, 3])
        cross = coeff_ref[0, k, 2] + u * coeff_ref[0, k, 4]
        for lane in range(0, cols, 256):
            horizontal = dot(vert[k], band[:, lane : lane + 256])
            for part in range(0, 256, 128):
                at = lane + part
                v = (
                    2.0 * (lax.broadcasted_iota(jnp.int32, (1, 128), 1) + at).astype(F32)
                    / (cols - 1)
                    - 1.0
                )
                weight = row_part + cross * v + coeff_ref[0, k, 5] * (v * v)
                acc[:, at : at + 128] += weight * horizontal[:, part : part + 128]
        return 0

    lax.fori_loop(0, bases, one_basis, 0)
    xpad[MARGIN : rows + MARGIN, :] = acc[...].astype(BF16)
    lead = LTAPS // 2 - 1
    row_band = toeplitz(lrow_ref[pl.ds(phase_ref[0, 0], 1), :], RB, MARGIN - lead).astype(BF16)
    for b in range(blocks):
        vert[0, b * RB : (b + 1) * RB, :] = dot(row_band, xpad[b * RB : b * RB + window, :]).astype(
            BF16
        )
    circulant = toeplitz(
        lcol_ref[pl.ds(phase_ref[0, 1], 1), :], lcol_ref.shape[1], -(LTAPS - 1 - lead)
    )
    fill_column_band(band, circulant, LTAPS - 1 - lead)
    warped = dot(vert[0], band[...])
    weight = jnp.where((mask_ref[...] & 7) != 0, vw_ref[0], 0.0)
    send_slots(rows_ref, (weight * warped).astype(BF16), outs)


def coadd_kernel(count, start_ref, *refs):
    flux, weight, out_ref = refs[:count], refs[count : 2 * count], refs[2 * count]
    cap, rows = flux[0].shape[0], out_ref.shape[0]
    gap = lax.broadcasted_iota(jnp.int32, (rows, cap), 0) - lax.broadcasted_iota(
        jnp.int32, (rows, cap), 1
    )
    me, peers = lax.axis_index("sky"), lax.axis_size("sky")
    flux_sum = weight_sum = 0.0
    for o in range(count):
        put = jnp.where(gap == start_ref[lax.rem(me - o + peers, peers), o], 1.0, 0.0).astype(BF16)
        flux_sum += dot(put, flux[o][...])
        weight_sum += dot(put, weight[o][...])
    out_ref[...] = flux_sum / (1.0 + weight_sum)


def detect_kernel(co_ref, lo_ref, hi_ref, grow_ref, ghi_ref, glo_ref, out_ref, tall, stack, smooth,
                  band_hi, band_lo):
    q = pl.program_id(0)
    rows, cols = co_ref.shape
    window = RB + 2 * HALO
    blocks = rows // RB

    @pl.when(q == 0)
    def _():
        for s in range(NSCALE):
            tall[s * RB : (s + 1) * RB, :] = toeplitz(grow_ref[s : s + 1, :], RB, 0).astype(BF16)
        stack[3 * window :, :] = jnp.zeros((stack.shape[0] - 3 * window, cols), BF16)
        for b in range(blocks):
            top = lo_ref[...] if b == 0 else co_ref[b * RB - HALO : b * RB, :]
            end = (b + 1) * RB
            bottom = hi_ref[...] if b == blocks - 1 else co_ref[end : end + HALO, :]
            for at, part in ((0, top), (HALO, co_ref[b * RB : end, :]), (HALO + RB, bottom)):
                coarse = part.astype(BF16)
                fine = (part - coarse.astype(F32)).astype(BF16)
                size = part.shape[0]
                stack[at : at + size, :] = coarse
                stack[window + at : window + at + size, :] = fine
                stack[2 * window + at : 2 * window + at + size, :] = coarse
            for s in range(NSCALE):
                result = dot(tall[s * RB : (s + 1) * RB, :], stack[...])
                coarse = result.astype(BF16)
                smooth[s, b * RB : end, :cols] = coarse
                smooth[s, b * RB : end, cols:] = (result - coarse.astype(F32)).astype(BF16)

    for g_ref, band in ((ghi_ref, band_hi), (glo_ref, band_lo)):
        fill_column_band(
            band, toeplitz(g_ref[pl.ds(q, 1), :], g_ref.shape[1], -HALO), HALO
        )
    for lane in range(0, cols, 256):
        part = slice(lane, lane + 256)
        out_ref[:, part] = (
            dot(smooth[q, :, :cols], band_hi[:, part])
            + dot(smooth[q, :, cols:], band_hi[:, part])
            + dot(smooth[q, :, :cols], band_lo[:, part])
        )


def split_np(values):
    values = values.astype(np.float32)
    coarse = values.astype(ml_dtypes.bfloat16).astype(np.float32)
    return coarse, values - coarse


def vm(count):
    return [pl.BlockSpec(memory_space=pltpu.VMEM)] * count


def sm(count):
    return [pl.BlockSpec(memory_space=pltpu.SMEM)] * count


def shifted(x, by):
    peers = lax.axis_size("sky")
    return lax.ppermute(x, "sky", [(i, (i + by) % peers) for i in range(peers)])


def body(
    section_image,
    mask_plane,
    visit_weight,
    poly_coeff,
    shift_phase,
    piece_rows,
    piece_start,
    basis_vertical,
    basis_horizontal,
):
    rows, cols = section_image.shape
    pieces = piece_rows.shape[1]
    cap = 2 * rows // pieces
    bases, taps = basis_vertical.shape
    slot = jax.ShapeDtypeStruct((cap, cols), BF16)
    params = pltpu.CompilerParams(vmem_limit_bytes=LIMIT)

    weights = pl.pallas_call(
        weight_kernel,
        name="weight_slots",
        out_shape=[slot] * pieces,
        in_specs=sm(2) + vm(1),
        out_specs=vm(pieces),
        compiler_params=params,
    )(visit_weight, piece_rows, mask_plane)
    local_weight = weights[0]
    weights = [weights[0]] + [shifted(weights[o], o) for o in range(1, pieces)]

    table = lanczos_table().astype(np.float32).astype(ml_dtypes.bfloat16).astype(np.float32)
    lead = LTAPS // 2 - 1
    lan_row = padded_rows(
        table, RB + 2 * MARGIN, MARGIN - lead
    )
    lan_col = padded_rows(
        table[:, ::-1], 256, lead + 1 - LTAPS
    )
    fluxes = pl.pallas_call(
        warp_kernel,
        name="warp",
        out_shape=[slot] * pieces,
        in_specs=sm(4) + [pl.BlockSpec(memory_space=pl.ANY)] + vm(6),
        out_specs=vm(pieces),
        scratch_shapes=[
            VMEM((rows + 2 * MARGIN, cols), BF16),
            VMEM((bases, rows, cols), BF16),
            VMEM((cols, cols), BF16),
            VMEM((bases * RB, RB + 2 * MARGIN), BF16),
            VMEM((rows, cols), F32),
            VMEM((-(-bases // 16) * 16, 128), F32),
            VMEM((-(-bases // 16) * 16, RB + 2 * MARGIN), F32),
            VMEM((-(-bases // 16) * 16, 256), F32),
        ],
        compiler_params=params,
        cost_estimate=pl.CostEstimate(
            flops=4 * bases * rows * cols * cols, bytes_accessed=4 * rows * cols, transcendentals=0
        ),
    )(visit_weight, poly_coeff, shift_phase, piece_rows, local_weight, section_image, mask_plane,
      basis_vertical, basis_horizontal, jnp.asarray(lan_row), jnp.asarray(lan_col))
    fluxes = [fluxes[0]] + [shifted(fluxes[o], o) for o in range(1, pieces)]

    coadd = pl.pallas_call(
        functools.partial(coadd_kernel, pieces),
        name="coadd",
        out_shape=jax.ShapeDtypeStruct((rows, cols), F32),
        in_specs=sm(1) + vm(2 * pieces),
        out_specs=pl.BlockSpec(memory_space=pltpu.VMEM),
        compiler_params=params,
    )(piece_start, *fluxes, *weights)

    low = shifted(coadd[rows - HALO :], 1)
    high = shifted(coadd[:HALO], -1)
    offsets = np.arange(-HALO, HALO + 1)
    window = RB + 2 * HALO
    row_taps = np.zeros((NSCALE, 512), np.float32)
    col_hi = np.zeros((NSCALE, 256), np.float32)
    col_lo = np.zeros((NSCALE, 256), np.float32)
    count = 2 * HALO + 1
    for q in range(NSCALE):
        width = HALO * (q + 1) / (2.0 * NSCALE)
        gaussian = np.exp(-offsets * offsets / (2.0 * width * width))
        gaussian = gaussian / gaussian.sum()
        coarse, fine = split_np(gaussian)
        row_taps[q, :count] = coarse
        row_taps[q, window : window + count] = coarse
        row_taps[q, 2 * window : 2 * window + count] = fine
        col_hi[q, :count], col_lo[q, :count] = split_np(gaussian / (gaussian * gaussian).sum())
    whole = lambda shape: pl.BlockSpec(shape, lambda q: (0, 0))
    detection = pl.pallas_call(
        detect_kernel,
        name="detect",
        grid=(NSCALE,),
        out_shape=jax.ShapeDtypeStruct((NSCALE, rows, cols), F32),
        in_specs=[
            whole((rows, cols)),
            whole((HALO, cols)),
            whole((HALO, cols)),
            whole((NSCALE, 512)),
            whole((NSCALE, 256)),
            whole((NSCALE, 256)),
        ],
        out_specs=pl.BlockSpec((None, rows, cols), lambda q: (q, 0, 0)),
        scratch_shapes=[
            VMEM((NSCALE * RB, 512), BF16),
            VMEM((512, cols), BF16),
            VMEM((NSCALE, rows, 2 * cols), BF16),
            VMEM((cols, cols), BF16),
            VMEM((cols, cols), BF16),
        ],
        compiler_params=params,
    )(coadd, low, high, jnp.asarray(row_taps), jnp.asarray(col_hi), jnp.asarray(col_lo))
    return coadd, detection


def solution(mesh):
    return jax.shard_map(
        body,
        mesh=mesh,
        in_specs=(
            P(("grp", "sky"), None),
            P(("grp", "sky"), None),
            P(("grp", "sky")),
            P(("grp", "sky"), None, None),
            P(("grp", "sky"), None),
            P(("grp", "sky"), None),
            P("grp", None),
            P(),
            P(),
        ),
        out_specs=(P(("grp", "sky"), None), P(None, ("grp", "sky"), None)),
        check_vma=False,
    )
```

```python
import functools

import jax
import jax.numpy as jnp
import ml_dtypes
import numpy as np
from jax import lax
from jax.experimental import pallas as pl
from jax.experimental.pallas import tpu as pltpu
from jax.sharding import PartitionSpec as P

LTAPS = 6
PHASES = 32
HALO = 16
NSCALE = 5
RB = 128
MARGIN = 64
F32 = jnp.float32
BF16 = jnp.bfloat16
VMEM = pltpu.VMEM
LIMIT = 60 * 1024 * 1024


def dot(a, b):
    return jnp.dot(a, b, preferred_element_type=F32)


def lanczos_table():
    phase = np.arange(PHASES)[:, None] / PHASES
    offsets = np.arange(LTAPS)[None, :] - (LTAPS // 2 - 1) - phase
    values = np.sinc(offsets) * np.sinc(offsets / 3.0)
    return values / values.sum(1, keepdims=True)


def padded_rows(values, width, shift):
    lead = shift % 8
    return np.pad(values, ((0, 0), (lead, width - lead - values.shape[1])))


def toeplitz(row, rows, shift):
    wide = jnp.broadcast_to(row, (rows, row.shape[1]))
    return pltpu.roll(wide, shift // 8 * 8 % row.shape[1], 1, stride=1, stride_axis=0)


def fill_column_band(band_ref, circulant, reach):
    half = circulant.shape[0]
    gap = lax.broadcasted_iota(jnp.int32, (half, half), 1) - lax.broadcasted_iota(
        jnp.int32, (half, half), 0
    )
    zero = jnp.zeros_like(circulant)
    upper = jnp.where(gap <= reach - half, circulant, zero).astype(BF16)
    lower = jnp.where(gap >= half - reach, circulant, zero).astype(BF16)
    diag = jnp.where(jnp.abs(gap) <= reach, circulant, zero).astype(BF16)
    count = band_ref.shape[0] // half
    none = jnp.zeros((half, half), BF16)
    for a in range(count):
        for b in range(count):
            tile = diag if a == b else upper if b == a + 1 else lower if b == a - 1 else none
            band_ref[a * half : (a + 1) * half, b * half : (b + 1) * half] = tile


def fill_slots(rows_ref, plane, slots_ref):
    count, cap, rows = slots_ref.shape[0], slots_ref.shape[1], plane.shape[0]
    row = lax.broadcasted_iota(jnp.int32, (cap, rows), 0)
    gap = lax.broadcasted_iota(jnp.int32, (cap, rows), 1) - row
    begin = 0
    for o in range(count):
        live = rows_ref[0, o]
        pick = jnp.where((row < live) & (gap == begin), 1.0, 0.0).astype(BF16)
        slots_ref[o] = dot(pick, plane).astype(BF16)
        begin = begin + live


def spread_taps(raw_ref, pad_ref, out_ref, lead, step):
    count, taps = raw_ref.shape
    pad_ref[...] = jnp.zeros_like(pad_ref)
    pad_ref[:count, :taps] = raw_ref[...]
    shape = (pad_ref.shape[1], out_ref.shape[1])
    tap = lax.broadcasted_iota(jnp.int32, shape, 0)
    lane = lax.broadcasted_iota(jnp.int32, shape, 1)
    pick = jnp.where((lane == lead + step * tap) & (tap < taps), 1.0, 0.0).astype(BF16)
    out_ref[...] = dot(pad_ref[...].astype(BF16), pick)


def section_kernel(vw_ref, coeff_ref, phase_ref, rows_ref, start_ref, img_ref, mask_ref, rawv_ref,
                   rawh_ref, lrow_ref, lcol_ref, out_ref, low_ref, high_ref, xpad, vert, band, tall,
                   acc, pad, vt_ref, ht_ref, wsend, wrecv, fsend, frecv, hsend, hrecv, send_sem,
                   recv_sem):
    pieces, cap = wsend.shape[:2]
    me, peers = lax.axis_index("sky"), lax.axis_size("sky")

    def peer(by):
        return {"sky": lax.rem(me + by + peers, peers)}

    def remote(src, dst, slot, by):
        return pltpu.make_async_remote_copy(
            src_ref=src,
            dst_ref=dst,
            send_sem=send_sem.at[slot],
            recv_sem=recv_sem.at[slot],
            device_id=peer(by),
            device_id_type=pl.DeviceIdType.MESH,
        )

    barrier = pltpu.get_barrier_semaphore()
    for o in range(1, pieces):
        for by in (o, -o):
            pl.semaphore_signal(
                barrier, inc=1, device_id=peer(by), device_id_type=pl.DeviceIdType.MESH
            )
    weight = jnp.where((mask_ref[...] & 7) != 0, vw_ref[0], 0.0)
    fill_slots(rows_ref, weight.astype(BF16), wsend)
    bases, taps = rawv_ref.shape
    rows, cols = img_ref.shape
    half_width = taps // 2
    spread_taps(rawv_ref, pad, vt_ref, (MARGIN - half_width) % 8, 1)
    spread_taps(rawh_ref, pad, ht_ref, (half_width + 1 - taps) % 8 + taps - 1, -1)
    blocks = rows // RB
    window = RB + 2 * MARGIN
    pl.semaphore_wait(barrier, 2 * (pieces - 1))
    weight_copies = [remote(wsend.at[o], wrecv.at[o - 1], o - 1, o) for o in range(1, pieces)]
    for copy in reversed(weight_copies):
        copy.start()
    xpad[:MARGIN, :] = jnp.zeros((MARGIN, cols), BF16)
    xpad[rows + MARGIN :, :] = jnp.zeros((MARGIN, cols), BF16)
    xpad[MARGIN : rows + MARGIN, :] = img_ref[...]
    acc[...] = jnp.zeros_like(acc)
    for k in range(bases):
        tall[k * RB : (k + 1) * RB, :] = toeplitz(
            vt_ref[k : k + 1, :], RB, MARGIN - half_width
        ).astype(BF16)
    for b in range(blocks):
        for k in range(bases):
            vert[k, b * RB : (b + 1) * RB, :] = dot(
                tall[k * RB : (k + 1) * RB, :], xpad[b * RB : b * RB + window, :]
            ).astype(BF16)
    u = 2.0 * lax.broadcasted_iota(jnp.int32, (rows, 128), 0).astype(F32) / (rows - 1) - 1.0

    def one_basis(k, _):
        circulant = toeplitz(ht_ref[pl.ds(k, 1), :], ht_ref.shape[1], -(taps - 1 - half_width))
        fill_column_band(band, circulant, half_width)
        row_part = coeff_ref[0, k, 0] + u * (coeff_ref[0, k, 1] + u * coeff_ref[0, k, 3])
        cross = coeff_ref[0, k, 2] + u * coeff_ref[0, k, 4]
        for lane in range(0, cols, 256):
            horizontal = dot(vert[k], band[:, lane : lane + 256])
            for part in range(0, 256, 128):
                at = lane + part
                v = (
                    2.0 * (lax.broadcasted_iota(jnp.int32, (1, 128), 1) + at).astype(F32)
                    / (cols - 1)
                    - 1.0
                )
                weight = row_part + cross * v + coeff_ref[0, k, 5] * (v * v)
                acc[:, at : at + 128] += weight * horizontal[:, part : part + 128]
        return 0

    lax.fori_loop(0, bases, one_basis, 0)
    xpad[MARGIN : rows + MARGIN, :] = acc[...].astype(BF16)
    lead = LTAPS // 2 - 1
    row_band = toeplitz(lrow_ref[pl.ds(phase_ref[0, 0], 1), :], RB, MARGIN - lead).astype(BF16)
    for b in range(blocks):
        vert[0, b * RB : (b + 1) * RB, :] = dot(row_band, xpad[b * RB : b * RB + window, :]).astype(
            BF16
        )
    circulant = toeplitz(
        lcol_ref[pl.ds(phase_ref[0, 1], 1), :], lcol_ref.shape[1], -(LTAPS - 1 - lead)
    )
    fill_column_band(band, circulant, LTAPS - 1 - lead)
    warped = dot(vert[0], band[...])
    weight = jnp.where((mask_ref[...] & 7) != 0, vw_ref[0], 0.0)
    fill_slots(rows_ref, (weight * warped).astype(BF16), fsend)
    first = pieces - 1
    flux_copies = [remote(fsend.at[o], frecv.at[o - 1], first + o - 1, o) for o in range(1, pieces)]
    for copy in reversed(flux_copies):
        copy.start()

    gap = lax.broadcasted_iota(jnp.int32, (rows, cap), 0) - lax.broadcasted_iota(
        jnp.int32, (rows, cap), 1
    )

    def placed(o, plane):
        put = jnp.where(gap == start_ref[lax.rem(me - o + peers, peers), o], 1.0, 0.0)
        return dot(put.astype(BF16), plane)

    acc[...] = placed(0, wsend[0])
    for o in range(1, pieces):
        weight_copies[o - 1].wait()
        acc[...] += placed(o, wrecv[o - 1])
    out_ref[...] = placed(0, fsend[0])
    for o in range(1, pieces):
        flux_copies[o - 1].wait()
        out_ref[...] += placed(o, frecv[o - 1])
    out_ref[...] = out_ref[...] / (1.0 + acc[...])
    hsend[0] = out_ref[rows - HALO :, :]
    hsend[1] = out_ref[:HALO, :]
    slot = 2 * first
    up, down = (remote(hsend.at[i], hrecv.at[i], slot + i, by) for i, by in ((0, 1), (1, -1)))
    up.start()
    down.start()
    up.wait()
    down.wait()
    low_ref[...] = hrecv[0]
    high_ref[...] = hrecv[1]


def detect_kernel(co_ref, lo_ref, hi_ref, grow_ref, ghi_ref, glo_ref, out_ref, tall, stack, smooth,
                  band_hi, band_lo):
    q = pl.program_id(0)
    rows, cols = co_ref.shape
    window = RB + 2 * HALO
    blocks = rows // RB

    @pl.when(q == 0)
    def _():
        for s in range(NSCALE):
            tall[s * RB : (s + 1) * RB, :] = toeplitz(grow_ref[s : s + 1, :], RB, 0).astype(BF16)
        stack[3 * window :, :] = jnp.zeros((stack.shape[0] - 3 * window, cols), BF16)
        for b in range(blocks):
            top = lo_ref[...] if b == 0 else co_ref[b * RB - HALO : b * RB, :]
            end = (b + 1) * RB
            bottom = hi_ref[...] if b == blocks - 1 else co_ref[end : end + HALO, :]
            for at, part in ((0, top), (HALO, co_ref[b * RB : end, :]), (HALO + RB, bottom)):
                coarse = part.astype(BF16)
                fine = (part - coarse.astype(F32)).astype(BF16)
                size = part.shape[0]
                stack[at : at + size, :] = coarse
                stack[window + at : window + at + size, :] = fine
                stack[2 * window + at : 2 * window + at + size, :] = coarse
            for s in range(NSCALE):
                result = dot(tall[s * RB : (s + 1) * RB, :], stack[...])
                coarse = result.astype(BF16)
                smooth[s, b * RB : end, :cols] = coarse
                smooth[s, b * RB : end, cols:] = (result - coarse.astype(F32)).astype(BF16)

    for g_ref, band in ((ghi_ref, band_hi), (glo_ref, band_lo)):
        fill_column_band(
            band, toeplitz(g_ref[pl.ds(q, 1), :], g_ref.shape[1], -HALO), HALO
        )
    for lane in range(0, cols, 256):
        part = slice(lane, lane + 256)
        out_ref[:, part] = (
            dot(smooth[q, :, :cols], band_hi[:, part])
            + dot(smooth[q, :, cols:], band_hi[:, part])
            + dot(smooth[q, :, :cols], band_lo[:, part])
        )


def split_np(values):
    values = values.astype(np.float32)
    coarse = values.astype(ml_dtypes.bfloat16).astype(np.float32)
    return coarse, values - coarse


def vm(count):
    return [pl.BlockSpec(memory_space=pltpu.VMEM)] * count


def sm(count):
    return [pl.BlockSpec(memory_space=pltpu.SMEM)] * count


def body(
    section_image,
    mask_plane,
    visit_weight,
    poly_coeff,
    shift_phase,
    piece_rows,
    piece_start,
    basis_vertical,
    basis_horizontal,
):
    rows, cols = section_image.shape
    pieces = piece_rows.shape[1]
    cap = 2 * rows // pieces
    bases, taps = basis_vertical.shape
    params = pltpu.CompilerParams(vmem_limit_bytes=LIMIT)

    table = lanczos_table().astype(np.float32).astype(ml_dtypes.bfloat16).astype(np.float32)
    lead = LTAPS // 2 - 1
    lan_row = padded_rows(
        table, RB + 2 * MARGIN, MARGIN - lead
    )
    lan_col = padded_rows(
        table[:, ::-1], 256, lead + 1 - LTAPS
    )
    basis_rows = -(-bases // 16) * 16
    slots = 2 * (pieces - 1) + 2
    coadd, low, high = pl.pallas_call(
        section_kernel,
        name="section",
        out_shape=[
            jax.ShapeDtypeStruct((rows, cols), F32),
            jax.ShapeDtypeStruct((HALO, cols), F32),
            jax.ShapeDtypeStruct((HALO, cols), F32),
        ],
        in_specs=sm(5) + vm(6),
        out_specs=vm(3),
        scratch_shapes=[
            VMEM((rows + 2 * MARGIN, cols), BF16),
            VMEM((bases, rows, cols), BF16),
            VMEM((cols, cols), BF16),
            VMEM((bases * RB, RB + 2 * MARGIN), BF16),
            VMEM((rows, cols), F32),
            VMEM((basis_rows, 128), F32),
            VMEM((basis_rows, RB + 2 * MARGIN), F32),
            VMEM((basis_rows, 256), F32),
            VMEM((pieces, cap, cols), BF16),
            VMEM((pieces - 1, cap, cols), BF16),
            VMEM((pieces, cap, cols), BF16),
            VMEM((pieces - 1, cap, cols), BF16),
            VMEM((2, HALO, cols), F32),
            VMEM((2, HALO, cols), F32),
            pltpu.SemaphoreType.DMA((slots,)),
            pltpu.SemaphoreType.DMA((slots,)),
        ],
        compiler_params=pltpu.CompilerParams(
            vmem_limit_bytes=LIMIT, collective_id=0, has_side_effects=True
        ),
    )(visit_weight, poly_coeff, shift_phase, piece_rows, piece_start, section_image, mask_plane,
      basis_vertical, basis_horizontal, jnp.asarray(lan_row), jnp.asarray(lan_col))

    offsets = np.arange(-HALO, HALO + 1)
    window = RB + 2 * HALO
    row_taps = np.zeros((NSCALE, 512), np.float32)
    col_hi = np.zeros((NSCALE, 256), np.float32)
    col_lo = np.zeros((NSCALE, 256), np.float32)
    count = 2 * HALO + 1
    for q in range(NSCALE):
        width = HALO * (q + 1) / (2.0 * NSCALE)
        gaussian = np.exp(-offsets * offsets / (2.0 * width * width))
        gaussian = gaussian / gaussian.sum()
        coarse, fine = split_np(gaussian)
        row_taps[q, :count] = coarse
        row_taps[q, window : window + count] = coarse
        row_taps[q, 2 * window : 2 * window + count] = fine
        col_hi[q, :count], col_lo[q, :count] = split_np(gaussian / (gaussian * gaussian).sum())
    whole = lambda shape: pl.BlockSpec(shape, lambda q: (0, 0))
    detection = pl.pallas_call(
        detect_kernel,
        name="detect",
        grid=(NSCALE,),
        out_shape=jax.ShapeDtypeStruct((NSCALE, rows, cols), F32),
        in_specs=[
            whole((rows, cols)),
            whole((HALO, cols)),
            whole((HALO, cols)),
            whole((NSCALE, 512)),
            whole((NSCALE, 256)),
            whole((NSCALE, 256)),
        ],
        out_specs=pl.BlockSpec((None, rows, cols), lambda q: (q, 0, 0)),
        scratch_shapes=[
            VMEM((NSCALE * RB, 512), BF16),
            VMEM((512, cols), BF16),
            VMEM((NSCALE, rows, 2 * cols), BF16),
            VMEM((cols, cols), BF16),
            VMEM((cols, cols), BF16),
        ],
        compiler_params=params,
    )(coadd, low, high, jnp.asarray(row_taps), jnp.asarray(col_hi), jnp.asarray(col_lo))
    return coadd, detection


def solution(mesh):
    return jax.shard_map(
        body,
        mesh=mesh,
        in_specs=(
            P(("grp", "sky"), None),
            P(("grp", "sky"), None),
            P(("grp", "sky")),
            P(("grp", "sky"), None, None),
            P(("grp", "sky"), None),
            P(("grp", "sky"), None),
            P("grp", None),
            P(),
            P(),
        ),
        out_specs=(P(("grp", "sky"), None), P(None, ("grp", "sky"), None)),
        check_vma=False,
    )
```

```python
import functools

import jax
import jax.numpy as jnp
import ml_dtypes
import numpy as np
from jax import lax
from jax.experimental import pallas as pl
from jax.experimental.pallas import tpu as pltpu
from jax.sharding import PartitionSpec as P

LTAPS = 6
PHASES = 32
HALO = 16
NSCALE = 5
RB = 128
MARGIN = 64
F32 = jnp.float32
BF16 = jnp.bfloat16
VMEM = pltpu.VMEM
LIMIT = 60 * 1024 * 1024


def dot(a, b):
    return jnp.dot(a, b, preferred_element_type=F32)


def lanczos_table():
    phase = np.arange(PHASES)[:, None] / PHASES
    offsets = np.arange(LTAPS)[None, :] - (LTAPS // 2 - 1) - phase
    values = np.sinc(offsets) * np.sinc(offsets / 3.0)
    return values / values.sum(1, keepdims=True)


def padded_rows(values, width, shift):
    lead = shift % 8
    return np.pad(values, ((0, 0), (lead, width - lead - values.shape[1])))


def toeplitz(row, rows, shift):
    wide = jnp.broadcast_to(row, (rows, row.shape[1]))
    return pltpu.roll(wide, shift // 8 * 8 % row.shape[1], 1, stride=1, stride_axis=0)


def fill_column_band(band_ref, circulant, reach):
    half = circulant.shape[0]
    gap = lax.broadcasted_iota(jnp.int32, (half, half), 1) - lax.broadcasted_iota(
        jnp.int32, (half, half), 0
    )
    zero = jnp.zeros_like(circulant)
    upper = jnp.where(gap <= reach - half, circulant, zero).astype(BF16)
    lower = jnp.where(gap >= half - reach, circulant, zero).astype(BF16)
    diag = jnp.where(jnp.abs(gap) <= reach, circulant, zero).astype(BF16)
    count = band_ref.shape[0] // half
    none = jnp.zeros((half, half), BF16)
    for a in range(count):
        for b in range(count):
            tile = diag if a == b else upper if b == a + 1 else lower if b == a - 1 else none
            band_ref[a * half : (a + 1) * half, b * half : (b + 1) * half] = tile


def fill_slots(rows_ref, plane, slots_ref):
    count, cap, rows = slots_ref.shape[0], slots_ref.shape[1], plane.shape[0]
    row = lax.broadcasted_iota(jnp.int32, (cap, rows), 0)
    gap = lax.broadcasted_iota(jnp.int32, (cap, rows), 1) - row
    begin = 0
    for o in range(count):
        live = rows_ref[0, o]
        pick = jnp.where((row < live) & (gap == begin), 1.0, 0.0).astype(BF16)
        slots_ref[o] = dot(pick, plane).astype(BF16)
        begin = begin + live


def spread_taps(raw_ref, pad_ref, out_ref, lead, step):
    count, taps = raw_ref.shape
    pad_ref[...] = jnp.zeros_like(pad_ref)
    pad_ref[:count, :taps] = raw_ref[...]
    shape = (pad_ref.shape[1], out_ref.shape[1])
    tap = lax.broadcasted_iota(jnp.int32, shape, 0)
    lane = lax.broadcasted_iota(jnp.int32, shape, 1)
    pick = jnp.where((lane == lead + step * tap) & (tap < taps), 1.0, 0.0).astype(BF16)
    out_ref[...] = dot(pad_ref[...].astype(BF16), pick)


def section_kernel(vw_ref, coeff_ref, phase_ref, rows_ref, start_ref, img_ref, mask_ref, rawv_ref,
                   rawh_ref, lrow_ref, lcol_ref, out_ref, low_ref, high_ref, xpad, vert, band, tall,
                   acc, pad, vt_ref, ht_ref, wsend, wrecv, fsend, frecv, hsend, hrecv, send_sem,
                   recv_sem):
    pieces, cap = wsend.shape[:2]
    me, peers = lax.axis_index("sky"), lax.axis_size("sky")

    def peer(by):
        return {"sky": lax.rem(me + by + peers, peers)}

    def remote(src, dst, slot, by):
        return pltpu.make_async_remote_copy(
            src_ref=src,
            dst_ref=dst,
            send_sem=send_sem.at[slot],
            recv_sem=recv_sem.at[slot],
            device_id=peer(by),
            device_id_type=pl.DeviceIdType.MESH,
        )

    barrier = pltpu.get_barrier_semaphore()
    for o in range(1, pieces):
        for by in (o, -o):
            pl.semaphore_signal(
                barrier, inc=1, device_id=peer(by), device_id_type=pl.DeviceIdType.MESH
            )
    weight = jnp.where((mask_ref[...] & 7) != 0, vw_ref[0], 0.0)
    fill_slots(rows_ref, weight.astype(BF16), wsend)
    bases, taps = rawv_ref.shape
    rows, cols = img_ref.shape
    half_width = taps // 2
    spread_taps(rawv_ref, pad, vt_ref, (MARGIN - half_width) % 8, 1)
    spread_taps(rawh_ref, pad, ht_ref, (half_width + 1 - taps) % 8 + taps - 1, -1)
    blocks = rows // RB
    window = RB + 2 * MARGIN
    pl.semaphore_wait(barrier, 2 * (pieces - 1))
    weight_copies = [remote(wsend.at[o], wrecv.at[o - 1], o - 1, o) for o in range(1, pieces)]
    for copy in reversed(weight_copies):
        copy.start()
    xpad[:MARGIN, :] = jnp.zeros((MARGIN, cols), BF16)
    xpad[rows + MARGIN :, :] = jnp.zeros((MARGIN, cols), BF16)
    xpad[MARGIN : rows + MARGIN, :] = img_ref[...]
    acc[...] = jnp.zeros_like(acc)
    for k in range(bases):
        tall[k * RB : (k + 1) * RB, :] = toeplitz(
            vt_ref[k : k + 1, :], RB, MARGIN - half_width
        ).astype(BF16)
    for b in range(blocks):
        for k in range(bases):
            vert[k, b * RB : (b + 1) * RB, :] = dot(
                tall[k * RB : (k + 1) * RB, :], xpad[b * RB : b * RB + window, :]
            ).astype(BF16)
    u = 2.0 * lax.broadcasted_iota(jnp.int32, (rows, 128), 0).astype(F32) / (rows - 1) - 1.0

    def one_basis(k, _):
        circulant = toeplitz(ht_ref[pl.ds(k, 1), :], ht_ref.shape[1], -(taps - 1 - half_width))
        fill_column_band(band, circulant, half_width)
        row_part = coeff_ref[0, 0, k] + u * (coeff_ref[0, 1, k] + u * coeff_ref[0, 3, k])
        cross = coeff_ref[0, 2, k] + u * coeff_ref[0, 4, k]
        for lane in range(0, cols, 256):
            horizontal = dot(vert[k], band[:, lane : lane + 256])
            for part in range(0, 256, 128):
                at = lane + part
                v = (
                    2.0 * (lax.broadcasted_iota(jnp.int32, (1, 128), 1) + at).astype(F32)
                    / (cols - 1)
                    - 1.0
                )
                weight = row_part + cross * v + coeff_ref[0, 5, k] * (v * v)
                acc[:, at : at + 128] += weight * horizontal[:, part : part + 128]
        return 0

    lax.fori_loop(0, bases, one_basis, 0)
    xpad[MARGIN : rows + MARGIN, :] = acc[...].astype(BF16)
    lead = LTAPS // 2 - 1
    row_band = toeplitz(lrow_ref[pl.ds(phase_ref[0, 0], 1), :], RB, MARGIN - lead).astype(BF16)
    for b in range(blocks):
        vert[0, b * RB : (b + 1) * RB, :] = dot(row_band, xpad[b * RB : b * RB + window, :]).astype(
            BF16
        )
    circulant = toeplitz(
        lcol_ref[pl.ds(phase_ref[0, 1], 1), :], lcol_ref.shape[1], -(LTAPS - 1 - lead)
    )
    fill_column_band(band, circulant, LTAPS - 1 - lead)
    warped = dot(vert[0], band[...])
    weight = jnp.where((mask_ref[...] & 7) != 0, vw_ref[0], 0.0)
    fill_slots(rows_ref, (weight * warped).astype(BF16), fsend)
    first = pieces - 1
    flux_copies = [remote(fsend.at[o], frecv.at[o - 1], first + o - 1, o) for o in range(1, pieces)]
    for copy in reversed(flux_copies):
        copy.start()

    gap = lax.broadcasted_iota(jnp.int32, (rows, cap), 0) - lax.broadcasted_iota(
        jnp.int32, (rows, cap), 1
    )

    def placed(o, plane):
        put = jnp.where(gap == start_ref[o, lax.rem(me - o + peers, peers)], 1.0, 0.0)
        return dot(put.astype(BF16), plane)

    acc[...] = placed(0, wsend[0])
    for o in range(1, pieces):
        weight_copies[o - 1].wait()
        acc[...] += placed(o, wrecv[o - 1])
    out_ref[...] = placed(0, fsend[0])
    for o in range(1, pieces):
        flux_copies[o - 1].wait()
        out_ref[...] += placed(o, frecv[o - 1])
    out_ref[...] = out_ref[...] / (1.0 + acc[...])
    hsend[0] = out_ref[rows - HALO :, :]
    hsend[1] = out_ref[:HALO, :]
    slot = 2 * first
    up, down = (remote(hsend.at[i], hrecv.at[i], slot + i, by) for i, by in ((0, 1), (1, -1)))
    up.start()
    down.start()
    up.wait()
    down.wait()
    low_ref[...] = hrecv[0]
    high_ref[...] = hrecv[1]


def detect_kernel(co_ref, lo_ref, hi_ref, grow_ref, ghi_ref, glo_ref, same_ref, out_ref, tall, stack,
                  smooth, band_hi, band_lo, sem):
    q = pl.program_id(0)
    rows, cols = co_ref.shape
    window = RB + 2 * HALO
    blocks = rows // RB
    keep = pltpu.make_async_copy(co_ref, same_ref, sem)

    @pl.when(q == 0)
    def _():
        keep.start()
        for s in range(NSCALE):
            tall[s * RB : (s + 1) * RB, :] = toeplitz(grow_ref[s : s + 1, :], RB, 0).astype(BF16)
        stack[3 * window :, :] = jnp.zeros((stack.shape[0] - 3 * window, cols), BF16)
        for b in range(blocks):
            top = lo_ref[...] if b == 0 else co_ref[b * RB - HALO : b * RB, :]
            end = (b + 1) * RB
            bottom = hi_ref[...] if b == blocks - 1 else co_ref[end : end + HALO, :]
            for at, part in ((0, top), (HALO, co_ref[b * RB : end, :]), (HALO + RB, bottom)):
                coarse = part.astype(BF16)
                fine = (part - coarse.astype(F32)).astype(BF16)
                size = part.shape[0]
                stack[at : at + size, :] = coarse
                stack[window + at : window + at + size, :] = fine
                stack[2 * window + at : 2 * window + at + size, :] = coarse
            for s in range(NSCALE):
                result = dot(tall[s * RB : (s + 1) * RB, :], stack[...])
                coarse = result.astype(BF16)
                smooth[s, b * RB : end, :cols] = coarse
                smooth[s, b * RB : end, cols:] = (result - coarse.astype(F32)).astype(BF16)

    for g_ref, band in ((ghi_ref, band_hi), (glo_ref, band_lo)):
        fill_column_band(
            band, toeplitz(g_ref[pl.ds(q, 1), :], g_ref.shape[1], -HALO), HALO
        )
    for lane in range(0, cols, 256):
        part = slice(lane, lane + 256)
        out_ref[:, part] = (
            dot(smooth[q, :, :cols], band_hi[:, part])
            + dot(smooth[q, :, cols:], band_hi[:, part])
            + dot(smooth[q, :, :cols], band_lo[:, part])
        )

    @pl.when(q == pl.num_programs(0) - 1)
    def _():
        keep.wait()


def split_np(values):
    values = values.astype(np.float32)
    coarse = values.astype(ml_dtypes.bfloat16).astype(np.float32)
    return coarse, values - coarse


def vm(count):
    return [pl.BlockSpec(memory_space=pltpu.VMEM)] * count


def sm(count):
    return [pl.BlockSpec(memory_space=pltpu.SMEM)] * count


def body(
    section_image,
    mask_plane,
    visit_weight,
    poly_coeff,
    shift_phase,
    piece_rows,
    piece_start,
    basis_vertical,
    basis_horizontal,
):
    rows, cols = section_image.shape
    pieces = piece_rows.shape[1]
    cap = 2 * rows // pieces
    bases, taps = basis_vertical.shape
    params = pltpu.CompilerParams(vmem_limit_bytes=LIMIT)

    table = lanczos_table().astype(np.float32).astype(ml_dtypes.bfloat16).astype(np.float32)
    lead = LTAPS // 2 - 1
    lan_row = padded_rows(
        table, RB + 2 * MARGIN, MARGIN - lead
    )
    lan_col = padded_rows(
        table[:, ::-1], 256, lead + 1 - LTAPS
    )
    basis_rows = -(-bases // 16) * 16
    slots = 2 * (pieces - 1) + 2
    coadd, low, high = pl.pallas_call(
        section_kernel,
        name="section",
        out_shape=[
            jax.ShapeDtypeStruct((rows, cols), F32),
            jax.ShapeDtypeStruct((HALO, cols), F32),
            jax.ShapeDtypeStruct((HALO, cols), F32),
        ],
        in_specs=sm(5) + vm(6),
        out_specs=vm(3),
        scratch_shapes=[
            VMEM((rows + 2 * MARGIN, cols), BF16),
            VMEM((bases, rows, cols), BF16),
            VMEM((cols, cols), BF16),
            VMEM((bases * RB, RB + 2 * MARGIN), BF16),
            VMEM((rows, cols), F32),
            VMEM((basis_rows, 128), F32),
            VMEM((basis_rows, RB + 2 * MARGIN), F32),
            VMEM((basis_rows, 256), F32),
            VMEM((pieces, cap, cols), BF16),
            VMEM((pieces - 1, cap, cols), BF16),
            VMEM((pieces, cap, cols), BF16),
            VMEM((pieces - 1, cap, cols), BF16),
            VMEM((2, HALO, cols), F32),
            VMEM((2, HALO, cols), F32),
            pltpu.SemaphoreType.DMA((slots,)),
            pltpu.SemaphoreType.DMA((slots,)),
        ],
        compiler_params=pltpu.CompilerParams(
            vmem_limit_bytes=LIMIT, collective_id=0, has_side_effects=True
        ),
    )(visit_weight, jnp.swapaxes(poly_coeff, 1, 2), shift_phase, piece_rows, piece_start.T, section_image, mask_plane,
      basis_vertical, basis_horizontal, jnp.asarray(lan_row), jnp.asarray(lan_col))

    offsets = np.arange(-HALO, HALO + 1)
    window = RB + 2 * HALO
    row_taps = np.zeros((NSCALE, 512), np.float32)
    col_hi = np.zeros((NSCALE, 256), np.float32)
    col_lo = np.zeros((NSCALE, 256), np.float32)
    count = 2 * HALO + 1
    for q in range(NSCALE):
        width = HALO * (q + 1) / (2.0 * NSCALE)
        gaussian = np.exp(-offsets * offsets / (2.0 * width * width))
        gaussian = gaussian / gaussian.sum()
        coarse, fine = split_np(gaussian)
        row_taps[q, :count] = coarse
        row_taps[q, window : window + count] = coarse
        row_taps[q, 2 * window : 2 * window + count] = fine
        col_hi[q, :count], col_lo[q, :count] = split_np(gaussian / (gaussian * gaussian).sum())
    whole = lambda shape: pl.BlockSpec(shape, lambda q: (0, 0))
    return pl.pallas_call(
        detect_kernel,
        name="detect",
        grid=(NSCALE,),
        out_shape=[
            jax.ShapeDtypeStruct((rows, cols), F32),
            jax.ShapeDtypeStruct((NSCALE, rows, cols), F32),
        ],
        in_specs=[
            whole((rows, cols)),
            whole((HALO, cols)),
            whole((HALO, cols)),
            whole((NSCALE, 512)),
            whole((NSCALE, 256)),
            whole((NSCALE, 256)),
        ],
        out_specs=[
            pl.BlockSpec(memory_space=pl.ANY),
            pl.BlockSpec((None, rows, cols), lambda q: (q, 0, 0)),
        ],
        scratch_shapes=[
            VMEM((NSCALE * RB, 512), BF16),
            VMEM((512, cols), BF16),
            VMEM((NSCALE, rows, 2 * cols), BF16),
            VMEM((cols, cols), BF16),
            VMEM((cols, cols), BF16),
            pltpu.SemaphoreType.DMA,
        ],
        compiler_params=params,
    )(coadd, low, high, jnp.asarray(row_taps), jnp.asarray(col_hi), jnp.asarray(col_lo))


def solution(mesh):
    return jax.shard_map(
        body,
        mesh=mesh,
        in_specs=(
            P(("grp", "sky"), None),
            P(("grp", "sky"), None),
            P(("grp", "sky")),
            P(("grp", "sky"), None, None),
            P(("grp", "sky"), None),
            P(("grp", "sky"), None),
            P("grp", None),
            P(),
            P(),
        ),
        out_specs=(P(("grp", "sky"), None), P(None, ("grp", "sky"), None)),
        check_vma=False,
    )
```
